32 devices in a mesh: dp: 4 (over x, core), seq: 8 (over z, y).
Axes of the slice: x: 2, y: 2, z: 4, core: 2. Of those that a mesh axis runs over, the one named last changes fastest.
Arguments:
- tile_embed: bfloat16 [4, 1024, 768], P('dp', 'seq'), may hold values from -6 to 6
- qkv_saved: bfloat16 [4, 1024, 1152], P('dp', 'seq'), may hold values from -8 to 8
- out_cotangent: bfloat16 [4, 1024, 768], P('dp', 'seq'), may hold values from -6 to 6
- qkv_weight: bfloat16 [768, 1152], replicated, may hold values from -0.21875 to 0.21875
- out_weight: bfloat16 [384, 768], replicated, may hold values from -0.3125 to 0.3125
- seg_length: int32 [8], replicated, may hold values from 128 to 1024, as said below
- dilation: int32 [8], replicated, may hold values from 1 to 4
- owner_map: int32 [4, 1024, 1], P('dp', 'seq'), may hold values from 0 to 7; in each aligned block of 128 rows (0 to 127, 128 to 255, ..., all dimensions but the last counted through in order) at most 32 rows name the same one
- tile_hidden: bfloat16 [4, 2048, 1536], P('dp', 'seq'), may hold values from -6 to 6
- tile_output: bfloat16 [4, 2048, 1536], P('dp', 'seq'), may hold values from -6 to 6
- embed_weight: bfloat16 [1536, 768], replicated, may hold values from -0.15625 to 0.15625
- proj_weight: bfloat16 [1536, 1536], replicated, may hold values from -0.15625 to 0.15625
Outputs:
- hidden_grad: bfloat16 [4, 2048, 1536], P('dp', 'seq')
- proj_weight_grad: float32 [1536, 1536], P(('dp', 'seq'))
- embed_weight_grad: float32 [1536, 768], P(('dp', 'seq'))
- qkv_weight_grad: float32 [768, 1152], P(('dp', 'seq'))
- out_weight_grad: float32 [384, 768], P(('dp', 'seq'))
The draws below stay inside these ranges and needn't reach their ends.
Inputs may be any that keep to these rules, and one draw needn't show every extreme that they name: `seg_length`: each is 128 times a power of two; some head has 1024. `owner_map`: among the 128 positions of one device, no device index is named more than 32 times.
All inputs are finite; a program needn't handle non-finite values.
Results may differ from the reference program's by a relative error of at most 0.015.
Values may be sent and summed in bfloat16 or wider, within the bound.
A program may use at most 128 MiB of HBM per device.

```python
import math
import jax
import jax.numpy as jnp
import numpy as np
from jax import lax

D_SLIDE = 768
HEADS = 8
HEAD_DIM = 48
D_TILE = 1536
TOK_DEV = 128
LENGTH = 1024
CAP = 32
SLOTS = 256
ROWS_ALL = 2048
N_DP = 4
N_SEQ = 8


def draw_qkv_saved(key, part):
    width = HEADS * HEAD_DIM
    shape = (N_DP, LENGTH, 3 * width)
    values_drawn = jnp.clip(jax.random.normal(key, shape, jnp.float32), -8.0, 8.0)
    return values_drawn.astype(jnp.bfloat16)


def draw_seg_length(key, part):
    levels = N_SEQ.bit_length()
    powers = jax.random.randint(jax.random.fold_in(key, 3), (HEADS,), 0, levels)
    powers = powers.at[0].set(levels - 1)
    powers = jax.random.permutation(jax.random.fold_in(key, 5), powers)
    return (jnp.left_shift(jnp.ones((HEADS,), jnp.int32), powers.astype(jnp.int32)) * TOK_DEV).astype(jnp.int32)


def set_ends(drawn, stream_key, smallest, largest):
    shape = drawn.shape
    spot = [jax.random.randint(jax.random.fold_in(stream_key, axis), (), 0, shape[axis]) for axis in range(len(shape))]
    drawn = drawn.at[tuple(spot)].set(smallest)
    longest = shape.index(max(shape))
    spot[longest] = (spot[longest] + 1) % shape[longest]
    return drawn.at[tuple(spot)].set(largest)


def shard_levels(key, extent, cuts, least, top_value):
    factor_of, own = 1.0, jax.random.fold_in(key, 6)
    for dim, parts in cuts:
        heights = jnp.exp(jax.random.uniform(jax.random.fold_in(own, dim), (parts,), jnp.float32, least / len(cuts), top_value / len(cuts)))
        factor_of = factor_of * jnp.repeat(heights, extent[dim] // parts).reshape([-1 if axis == dim else 1 for axis in range(len(extent))])
    return factor_of


def routed_block(key, own, number, rows, amount, top, limit, slope):
    ranking = jax.random.permutation(key, amount)
    crowded, common = load_shares(amount, rows * top, limit, slope, True), load_shares(amount, rows * top, limit, slope, False)
    places = jnp.arange(amount)

    def named(sizes, offset_by):
        used = int((sizes > 0).sum())
        fixed = max(1, used // 4)
        passed = fixed + (places - fixed + offset_by * (used - fixed)) % max(1, amount - fixed)
        return jnp.zeros((amount,), jnp.int32).at[ranking[jnp.where(places < fixed, places, passed)]].set(jnp.asarray(sizes, jnp.int32))

    sizes = jnp.where(number % 4 == 0, named(crowded, number // 4), named(common, number - number // 4 - 1))
    mixed = jax.random.permutation(jax.random.fold_in(own, 3), amount)
    donor, sink = mixed[0:amount // 2 * 2:2], mixed[1:amount // 2 * 2:2]
    room = jnp.minimum(sizes[donor] - 1, limit - sizes[sink]) // 2
    room = jnp.where((donor == ranking[0]) | (sink == ranking[0]) | (sizes[sink] == 0), 0, jnp.maximum(room, 0))
    passed = jax.random.randint(jax.random.fold_in(own, 4), (amount // 2,), 0, 1 << 20) % (room + 1)
    sizes = sizes.at[donor].add(-passed).at[sink].add(passed)
    labels = jnp.searchsorted(jnp.cumsum(sizes), jnp.arange(rows * top), side="right").astype(jnp.int32)
    grid = labels.reshape(top, rows).T
    grid = grid[jax.random.permutation(jax.random.fold_in(own, 1), rows)]
    offset_by = jax.random.randint(jax.random.fold_in(own, 2), (rows, 1), 0, top)
    return jnp.take_along_axis(grid, (jnp.arange(top)[None, :] + offset_by) % top, axis=1)


def load_shares(number_of, total, most, skew, full):
    portions = [(1 << 20) // math.isqrt(standing ** skew) + 1 for standing in range(1, number_of + 1)]
    largest = most if full else min(most, max(-(-total // number_of), total * portions[0] // sum(portions)))
    least = 1 if total - largest >= number_of - 1 else 0
    holding, rest = [largest] + [least] * (number_of - 1), total - largest - least * (number_of - 1)
    while rest > 0:
        free = [i for i in range(1, number_of) if holding[i] < largest] or [i for i in range(1, number_of) if holding[i] < most]
        pool, budget = sum([portions[i] for i in free]), rest
        for i in free:
            addition = min(most - holding[i], max(1, budget * portions[i] // pool), rest)
            holding[i] = holding[i] + addition
            rest = rest - addition
    return np.array(holding)


def noise(stream_key, dims, deviation, bound, shards=(), kind=jnp.bfloat16):
    gain = shard_levels(stream_key, dims, shards, -0.22, 0.18) if shards else 1.0
    drawn = jax.random.normal(stream_key, dims, jnp.float32) * deviation * gain
    return jnp.minimum(jnp.maximum(drawn, -bound), bound).astype(kind)


def setup_inputs(seed: int = 0) -> dict:
    key_list = jax.random.split(jax.random.key(seed), 13)
    tile_embed = noise(key_list[0], (N_DP, LENGTH, D_SLIDE), 1.0, 6.0, ((0, 4), (1, 8)))
    qkv_saved = draw_qkv_saved(jax.random.fold_in(key_list[12], 71), 0)
    out_cotangent = noise(key_list[2], (N_DP, LENGTH, D_SLIDE), 1.0, 6.0, ((0, 4), (1, 8)))
    qkv_weight = noise(key_list[3], (D_SLIDE, 3 * HEADS * HEAD_DIM), D_SLIDE ** -0.5, 0.21875)
    out_weight = noise(key_list[4], (HEADS * HEAD_DIM, D_SLIDE), (HEADS * HEAD_DIM) ** -0.5, 0.3125)
    seg_length = draw_seg_length(jax.random.fold_in(key_list[12], 71), 0)
    dilation = set_ends(jax.random.randint(key_list[6], (HEADS,), 1, 5), jax.random.fold_in(key_list[6], 1), 1, 4).astype(jnp.int32)
    owner_map_keys = jax.random.split(jax.random.fold_in(key_list[7], 1), N_DP * LENGTH // TOK_DEV)
    owner_map_turns = jax.random.permutation(jax.random.fold_in(key_list[7], 3), N_DP * LENGTH // TOK_DEV)
    owner_map = jax.vmap(lambda own, number: routed_block(jax.random.fold_in(key_list[7], 2), own, number, TOK_DEV, N_SEQ, 1, CAP, 2))(owner_map_keys, owner_map_turns).reshape((N_DP, LENGTH, 1))
    tile_hidden = noise(key_list[8], (N_DP, ROWS_ALL, D_TILE), 1.0, 6.0, ((0, 4), (1, 8)))
    tile_output = noise(key_list[9], (N_DP, ROWS_ALL, D_TILE), 1.0, 6.0, ((0, 4), (1, 8)))
    embed_weight = noise(key_list[10], (D_TILE, D_SLIDE), D_TILE ** -0.5, 0.15625)
    proj_weight = noise(key_list[11], (D_TILE, D_TILE), D_TILE ** -0.5, 0.15625)
    return dict(tile_embed=tile_embed, qkv_saved=qkv_saved, out_cotangent=out_cotangent, qkv_weight=qkv_weight, out_weight=out_weight, seg_length=seg_length, dilation=dilation, owner_map=owner_map, tile_hidden=tile_hidden, tile_output=tile_output, embed_weight=embed_weight, proj_weight=proj_weight)


def head_math(queries, keys_all, values_all, grads_out, span, stride, query_pos, key_pos, scaling):
    allowed = (query_pos[:, None] // span == key_pos[None, :] // span) & ((key_pos[None, :] - query_pos[:, None]) % stride == 0)
    scores = jnp.einsum("qd,kd->qk", queries, keys_all) * scaling
    scores = jnp.where(allowed, scores, -1e30)
    shifted = jnp.exp(scores - jnp.max(scores, axis=1, keepdims=True))
    probs_full = shifted / jnp.sum(shifted, axis=1, keepdims=True)
    probs_half = probs_full.astype(jnp.bfloat16).astype(jnp.float32)
    head_out = jnp.einsum("qk,kd->qd", probs_half, values_all)
    prob_grad = jnp.einsum("qd,kd->qk", grads_out, values_all)
    row_delta = jnp.sum(probs_full * prob_grad, axis=1, keepdims=True)
    score_grad = (probs_full * (prob_grad - row_delta) * scaling).astype(jnp.bfloat16).astype(jnp.float32)
    query_grad = jnp.einsum("qk,kd->qd", score_grad, keys_all)
    key_grad = jnp.einsum("qk,qd->kd", score_grad, queries)
    value_grad = jnp.einsum("qk,qd->kd", probs_half, grads_out)
    return head_out, query_grad, key_grad, value_grad


def split_heads(block, head_count, head_width):
    return block.reshape(block.shape[0], head_count, head_width).transpose(1, 0, 2)


def merge_heads(block):
    return block.transpose(1, 0, 2).reshape(block.shape[1], block.shape[0] * block.shape[2])


def slide_pass(embed_rows, saved, cotangent, qkv_weight, out_weight, seg_length, dilation):
    head_count = seg_length.shape[0]
    heads_width = out_weight.shape[0]
    head_width = heads_width // head_count
    length = saved.shape[0]
    scaling = head_width ** -0.5
    grads_out = jnp.dot(cotangent, out_weight.T, preferred_element_type=jnp.float32).astype(jnp.bfloat16)
    queries = split_heads(saved[:, :heads_width].astype(jnp.float32), head_count, head_width)
    keys_all = split_heads(saved[:, heads_width:2 * heads_width].astype(jnp.float32), head_count, head_width)
    values_all = split_heads(saved[:, 2 * heads_width:].astype(jnp.float32), head_count, head_width)
    grads_heads = split_heads(grads_out.astype(jnp.float32), head_count, head_width)
    key_pos = jnp.arange(length, dtype=jnp.int32)

    def block_step(carry, block_index):
        first_row = (block_index * TOK_DEV).astype(jnp.int32)
        query_pos = first_row + jnp.arange(TOK_DEV, dtype=jnp.int32)
        query_rows = lax.dynamic_slice_in_dim(queries, first_row, TOK_DEV, 1)
        grad_rows = lax.dynamic_slice_in_dim(grads_heads, first_row, TOK_DEV, 1)
        head_out, query_grad, key_grad, value_grad = jax.vmap(
            lambda qh, kh, vh, gh, span, stride: head_math(qh, kh, vh, gh, span, stride, query_pos, key_pos, scaling)
        )(query_rows, keys_all, values_all, grad_rows, seg_length, dilation)
        term = jnp.concatenate([merge_heads(key_grad), merge_heads(value_grad)], axis=1)
        rounded = lax.optimization_barrier(term.astype(jnp.bfloat16))
        return carry + rounded.astype(jnp.float32), (merge_heads(head_out), merge_heads(query_grad))

    start = jnp.zeros((length, 2 * heads_width), jnp.float32)
    summed, (outs, qgrads) = lax.scan(block_step, start, jnp.arange(N_SEQ, dtype=jnp.int32))
    attention = outs.reshape(length, heads_width).astype(jnp.bfloat16)
    query_grad = qgrads.reshape(length, heads_width)
    qkv_grad = jnp.concatenate([query_grad, summed], axis=1).astype(jnp.bfloat16)
    embed_grad = (cotangent.astype(jnp.float32) + jnp.dot(qkv_grad, qkv_weight.T, preferred_element_type=jnp.float32)).astype(jnp.bfloat16)
    qkv_term = jnp.dot(embed_rows.T, qkv_grad, preferred_element_type=jnp.float32)
    out_term = jnp.dot(attention.T, cotangent, preferred_element_type=jnp.float32)
    return embed_grad, qkv_term, out_term


def reference(tile_embed, qkv_saved, out_cotangent, qkv_weight, out_weight, seg_length, dilation, owner_map, tile_hidden, tile_output, embed_weight, proj_weight):
    length = qkv_saved.shape[1]
    hidden_list = []
    qkv_sum = jnp.zeros(qkv_weight.shape, jnp.float32)
    out_sum = jnp.zeros(out_weight.shape, jnp.float32)
    embed_sum = jnp.zeros(embed_weight.shape, jnp.float32)
    proj_sum = jnp.zeros(proj_weight.shape, jnp.float32)
    for slide in range(N_DP):
        embed_grad, qkv_term, out_term = slide_pass(tile_embed[slide], qkv_saved[slide], out_cotangent[slide], qkv_weight, out_weight, seg_length, dilation)
        qkv_sum = qkv_sum + qkv_term
        out_sum = out_sum + out_term
        destination = owner_map[slide, :, 0].astype(jnp.int32)
        blocked = destination.reshape(N_SEQ, TOK_DEV)
        onehot = (blocked[:, :, None] == jnp.arange(N_SEQ, dtype=jnp.int32)[None, None, :]).astype(jnp.int32)
        before = jnp.cumsum(onehot, axis=1) - onehot
        slot_rank = jnp.sum(before * onehot, axis=2).reshape(length)
        source = jnp.arange(length, dtype=jnp.int32) // TOK_DEV
        row_index = (destination * SLOTS + source * CAP + slot_rank).astype(jnp.int32)
        incoming = jnp.zeros((ROWS_ALL, embed_grad.shape[1]), jnp.bfloat16).at[row_index].set(embed_grad)
        tile_grad = jnp.dot(incoming, embed_weight.T, preferred_element_type=jnp.float32)
        hidden_list.append(jnp.dot(tile_grad.astype(jnp.bfloat16), proj_weight.T, preferred_element_type=jnp.float32).astype(jnp.bfloat16))
        embed_sum = embed_sum + jnp.dot(tile_output[slide].T, incoming, preferred_element_type=jnp.float32)
        proj_sum = proj_sum + jnp.dot(tile_hidden[slide].astype(jnp.float32).T, tile_grad, precision=lax.Precision.HIGHEST)
    return jnp.stack(hidden_list), proj_sum, embed_sum, qkv_sum, out_sum
```

```python
from functools import partial

import jax
import jax.numpy as jnp
from jax import lax
from jax.experimental import pallas as pl
from jax.experimental.pallas import tpu as pltpu
from jax.sharding import PartitionSpec as P


MESH = pl.DeviceIdType.MESH
BF16 = jnp.bfloat16
F32 = jnp.float32


def head_backward(pieces, query_pos, key_pos, scaling):
    queries, keys_all, values_all, grads_out, span, stride = pieces
    allowed = (query_pos[:, None] // span == key_pos[None, :] // span) & (
        (key_pos[None, :] - query_pos[:, None]) % stride == 0
    )
    scores = (
        jnp.einsum("qd,kd->qk", queries, keys_all, preferred_element_type=jnp.float32) * scaling
    )
    scores = jnp.where(allowed, scores, -1e30)
    shifted = jnp.exp(scores - jnp.max(scores, axis=1, keepdims=True))
    probs_full = shifted / jnp.sum(shifted, axis=1, keepdims=True)
    probs_half = probs_full.astype(jnp.bfloat16)
    head_out = jnp.einsum("qk,kd->qd", probs_half, values_all, preferred_element_type=jnp.float32)
    prob_grad = jnp.einsum("qd,kd->qk", grads_out, values_all, preferred_element_type=jnp.float32)
    row_delta = jnp.sum(probs_full * prob_grad, axis=1, keepdims=True)
    score_grad = (probs_full * (prob_grad - row_delta) * scaling).astype(jnp.bfloat16)
    query_grad = jnp.einsum("qk,kd->qd", score_grad, keys_all, preferred_element_type=jnp.float32)
    key_grad = jnp.einsum("qk,qd->kd", score_grad, queries, preferred_element_type=jnp.float32)
    value_grad = jnp.einsum("qk,qd->kd", probs_half, grads_out, preferred_element_type=jnp.float32)
    return (head_out, query_grad, key_grad, value_grad)


def local(
    tile_embed,
    qkv_saved,
    out_cotangent,
    qkv_weight,
    out_weight,
    seg_length,
    dilation,
    owner_map,
    tile_hidden,
    tile_output,
    embed_weight,
    proj_weight,
):
    head_count = seg_length.shape[0]
    heads_width = out_weight.shape[0]
    head_width = heads_width // head_count
    tokens_here = qkv_saved.shape[1]
    seq_count = lax.axis_size("seq")
    length = tokens_here * seq_count
    scaling = head_width ** (-0.5)
    saved = qkv_saved[0]
    cotangent = out_cotangent[0]
    embed_rows = tile_embed[0]

    def split_heads(block):
        return block.reshape(block.shape[0], head_count, head_width).transpose(1, 0, 2)

    def merge_heads(block):
        return block.transpose(1, 0, 2).reshape(block.shape[1], heads_width)

    key_value = lax.all_gather(saved[:, heads_width:], "seq", axis=0, tiled=True)
    grads_out = jnp.einsum(
        "td,cd->tc", cotangent, out_weight, preferred_element_type=jnp.float32
    ).astype(jnp.bfloat16)
    query_pos = lax.axis_index("seq") * tokens_here + jnp.arange(tokens_here, dtype=jnp.int32)
    key_pos = jnp.arange(length, dtype=jnp.int32)
    pieces = (
        split_heads(saved[:, :heads_width]),
        split_heads(key_value[:, :heads_width]),
        split_heads(key_value[:, heads_width:]),
        split_heads(grads_out),
        seg_length,
        dilation,
    )
    head_out, query_grad, key_grad, value_grad = lax.map(
        partial(head_backward, query_pos=query_pos, key_pos=key_pos, scaling=scaling), pieces
    )
    attention = merge_heads(head_out).astype(jnp.bfloat16)
    partials = jnp.concatenate([merge_heads(key_grad), merge_heads(value_grad)], axis=1)
    summed = lax.psum_scatter(
        partials.astype(jnp.bfloat16), "seq", scatter_dimension=0, tiled=True
    ).astype(jnp.float32)
    qkv_grad = jnp.concatenate([merge_heads(query_grad), summed], axis=1).astype(jnp.bfloat16)
    embed_grad = (
        cotangent.astype(jnp.float32)
        + jnp.einsum("tc,dc->td", qkv_grad, qkv_weight, preferred_element_type=jnp.float32)
    ).astype(jnp.bfloat16)
    columns = embed_rows
    qkv_sum = lax.psum_scatter(
        jnp.einsum("tc,tk->ck", columns, qkv_grad, preferred_element_type=jnp.float32),
        ("dp", "seq"),
        scatter_dimension=0,
        tiled=True,
    )
    columns = attention
    out_sum = lax.psum_scatter(
        jnp.einsum("tc,tk->ck", columns, cotangent, preferred_element_type=jnp.float32),
        ("dp", "seq"),
        scatter_dimension=0,
        tiled=True,
    )
    destination = owner_map[0, :, 0]
    capacity = tile_hidden.shape[1] // seq_count
    onehot = (destination[:, None] == jnp.arange(seq_count, dtype=jnp.int32)[None, :]).astype(
        jnp.int32
    )
    before = jnp.cumsum(onehot, axis=0) - onehot
    slot_index = destination * capacity + jnp.sum(before * onehot, axis=1)
    selector = (
        jnp.arange(seq_count * capacity, dtype=jnp.int32)[:, None] == slot_index[None, :]
    ).astype(jnp.bfloat16)
    outgoing = jnp.dot(selector, embed_grad, preferred_element_type=jnp.float32).astype(
        jnp.bfloat16
    )
    outgoing = outgoing.reshape(seq_count, capacity, embed_grad.shape[1])
    incoming = lax.all_to_all(outgoing, "seq", split_axis=0, concat_axis=0, tiled=True).reshape(
        seq_count * capacity, embed_grad.shape[1]
    )
    hidden_rows = tile_hidden[0]
    output_rows = tile_output[0]
    tile_grad = jnp.einsum("sd,ed->se", incoming, embed_weight, preferred_element_type=jnp.float32)
    grad_high = tile_grad.astype(jnp.bfloat16)
    hidden_grad = jnp.einsum(
        "se,fe->sf", grad_high, proj_weight, preferred_element_type=jnp.float32
    ).astype(jnp.bfloat16)[None]
    columns = output_rows
    embed_sum = lax.psum_scatter(
        jnp.einsum("sc,sd->cd", columns, incoming, preferred_element_type=jnp.float32),
        ("dp", "seq"),
        scatter_dimension=0,
        tiled=True,
    )
    columns = hidden_rows
    factor = lax.psum_scatter(
        jnp.einsum("sc,sd->cd", columns, incoming, preferred_element_type=jnp.float32),
        ("dp", "seq"),
        scatter_dimension=0,
        tiled=True,
    )
    proj_sum = jnp.dot(factor, embed_weight.astype(jnp.float32).T, precision=lax.Precision.HIGHEST)
    return (hidden_grad, proj_sum, embed_sum, qkv_sum, out_sum)


def greet(peers):
    barrier = pltpu.get_barrier_semaphore()
    for peer in peers:
        pl.semaphore_signal(barrier, inc=1, device_id=peer, device_id_type=MESH)
    pl.semaphore_wait(barrier, len(peers))


def swap_blocks(source, target, send_sems, recv_sems, count):
    me = lax.axis_index("seq")
    copies = []
    for step in range(1, count):
        peer = lax.rem(me + step, count)
        copy = pltpu.make_async_remote_copy(
            src_ref=source.at[peer],
            dst_ref=target.at[me],
            send_sem=send_sems.at[step - 1],
            recv_sem=recv_sems.at[step - 1],
            device_id=(lax.axis_index("dp"), peer),
            device_id_type=MESH,
        )
        copy.start()
        copies.append(copy)
    return copies


def seq_peers(count):
    me = lax.axis_index("seq")
    return [(lax.axis_index("dp"), lax.rem(me + step, count)) for step in range(1, count)]


def exchange_kernel(count, source, target, send_sems, recv_sems, local_sem):
    me = lax.axis_index("seq")
    greet(seq_peers(count))
    own = pltpu.make_async_copy(source.at[me], target.at[me], local_sem)
    own.start()
    copies = swap_blocks(source, target, send_sems, recv_sems, count)
    own.wait()
    for copy in copies:
        copy.wait()


def exchange(blocks):
    count = blocks.shape[0]
    return pl.pallas_call(
        partial(exchange_kernel, count),
        out_shape=jax.ShapeDtypeStruct(blocks.shape, blocks.dtype),
        in_specs=[pl.BlockSpec(memory_space=pltpu.VMEM)],
        out_specs=pl.BlockSpec(memory_space=pltpu.VMEM),
        scratch_shapes=[
            pltpu.SemaphoreType.DMA((count - 1,)),
            pltpu.SemaphoreType.DMA((count - 1,)),
            pltpu.SemaphoreType.DMA,
        ],
        compiler_params=pltpu.CompilerParams(collective_id=1, has_side_effects=True),
        name="tile_exchange",
    )(blocks)


def attention_kernel(
    count,
    width,
    scaling,
    source,
    id_column,
    id_row,
    result,
    arrived,
    outgoing,
    ids,
    keys_t,
    values_t,
    keys_n,
    values_n,
    key_total,
    value_total,
    send_sems,
    recv_sems,
    back_send,
    back_recv,
    local_sems,
):
    me = lax.axis_index("seq")
    tokens = source.shape[2]
    length = count * tokens
    greet(seq_peers(count))
    own = pltpu.make_async_copy(source.at[me], arrived.at[me], local_sems.at[0])
    own.start()
    copies = swap_blocks(source, arrived, send_sems, recv_sems, count)
    ids[...] = jnp.broadcast_to(id_column[...], (length, tokens))
    key_total[...] = jnp.zeros_like(key_total)
    value_total[...] = jnp.zeros_like(value_total)
    own.wait()
    for copy in copies:
        copy.wait()
    for block in range(count):
        lanes = slice(block * tokens, (block + 1) * tokens)
        key_block = arrived[block, width : 2 * width, :]
        value_block = arrived[block, 2 * width : 3 * width, :]
        keys_t[:, lanes] = key_block
        values_t[:, lanes] = value_block
        keys_n[lanes, :] = key_block.astype(F32).T.astype(BF16)
        values_n[lanes, :] = value_block.astype(F32).T.astype(BF16)

    def one_block(block, carry):
        queries = arrived[block, 0:width, :]
        grads = arrived[block, 3 * width : 4 * width, :]
        scores = jnp.dot(keys_n[...], queries, preferred_element_type=F32) * scaling
        scores = jnp.where(ids[...] == id_row[block], scores, -1e30)
        shifted = jnp.exp(scores - jnp.max(scores, axis=0, keepdims=True))
        probs = shifted * (1.0 / jnp.sum(shifted, axis=0, keepdims=True))
        probs_half = probs.astype(BF16)
        head_out = jnp.dot(values_t[...], probs_half, preferred_element_type=F32)
        prob_grad = jnp.dot(values_n[...], grads, preferred_element_type=F32)
        row_delta = jnp.sum(probs * prob_grad, axis=0, keepdims=True)
        score_grad = (probs * (prob_grad - row_delta) * scaling).astype(BF16)
        query_grad = jnp.dot(keys_t[...], score_grad, preferred_element_type=F32)
        last = (((1,), (1,)), ((), ()))
        key_total[...] += lax.dot_general(queries, score_grad, last, preferred_element_type=F32)
        value_total[...] += lax.dot_general(grads, probs_half, last, preferred_element_type=F32)
        outgoing[block, 0:width, :] = head_out.astype(BF16)
        outgoing[block, width : 2 * width, :] = query_grad.astype(BF16)
        return carry

    lax.fori_loop(0, count, one_block, 0)
    for block in range(count):
        lanes = slice(block * tokens, (block + 1) * tokens)
        outgoing[block, 2 * width : 3 * width, :] = key_total[:, lanes].astype(BF16)
        outgoing[block, 3 * width : 4 * width, :] = value_total[:, lanes].astype(BF16)
    own = pltpu.make_async_copy(outgoing.at[me], result.at[me], local_sems.at[1])
    own.start()
    copies = swap_blocks(outgoing, result, back_send, back_recv, count)
    own.wait()
    for copy in copies:
        copy.wait()


def attention_by_head(blocks, ids, width, scaling):
    count, _, tokens = blocks.shape
    length = count * tokens
    vmem = pl.BlockSpec(memory_space=pltpu.VMEM)
    sems = pltpu.SemaphoreType.DMA((count - 1,))
    return pl.pallas_call(
        partial(attention_kernel, count, width, scaling),
        out_shape=jax.ShapeDtypeStruct(blocks.shape, BF16),
        in_specs=[vmem] * 3,
        out_specs=vmem,
        scratch_shapes=[
            pltpu.VMEM(blocks.shape, BF16),
            pltpu.VMEM(blocks.shape, BF16),
            pltpu.VMEM((length, tokens), jnp.int32),
            pltpu.VMEM((width, length), BF16),
            pltpu.VMEM((width, length), BF16),
            pltpu.VMEM((length, width), BF16),
            pltpu.VMEM((length, width), BF16),
            pltpu.VMEM((width, length), F32),
            pltpu.VMEM((width, length), F32),
            sems,
            sems,
            sems,
            sems,
            pltpu.SemaphoreType.DMA((2,)),
        ],
        compiler_params=pltpu.CompilerParams(collective_id=0, has_side_effects=True),
        name="head_attention",
    )(blocks, ids[:, None], ids.reshape(count, 1, tokens))


def reduce_kernel(bit_counts, orders, *refs):
    streams = len(orders)
    bits = sum(bit_counts)
    dp_bits, seq_bits = bit_counts
    sources, results = refs[:streams], refs[streams : 2 * streams]
    held = refs[2 * streams : 3 * streams]
    landing = refs[3 * streams : 3 * streams + streams * bits]
    send_sems, recv_sems = refs[3 * streams + streams * bits :]
    dp, seq = lax.axis_index("dp"), lax.axis_index("seq")
    mine = [(dp // 2 ** (dp_bits - 1 - b)) % 2 for b in range(dp_bits)]
    mine += [(seq // 2 ** (seq_bits - 1 - b)) % 2 for b in range(seq_bits)]

    def partner(bit):
        if bit < dp_bits:
            return (dp + (1 - 2 * mine[bit]) * 2 ** (dp_bits - 1 - bit), seq)
        return (dp, seq + (1 - 2 * mine[bit]) * 2 ** (bits - 1 - bit))

    greet([partner(bit) for bit in range(bits)])
    copies = {}

    def start(stream, stage):
        order = orders[stream]
        done, now = order[:stage], order[stage]
        buffer = sources[stream] if stage == 0 else held[stream]
        index = []
        for bit in range(bits):
            if stage > 0 and bit == order[0]:
                continue
            if bit in done:
                index.append(mine[bit])
            elif bit == now:
                index.append(1 - mine[bit])
            else:
                index.append(slice(None))
        copy = pltpu.make_async_remote_copy(
            src_ref=buffer.at[tuple(index)],
            dst_ref=landing[stream * bits + stage],
            send_sem=send_sems.at[stream * bits + stage],
            recv_sem=recv_sems.at[stream * bits + stage],
            device_id=partner(now),
            device_id_type=MESH,
        )
        copy.start()
        copies[stream, stage] = copy

    def add(stream, stage):
        order = orders[stream]
        open_bits = [bit for bit in range(bits) if bit not in order[: stage + 1]]
        target = landing[stream * bits + stage]

        def place(step):
            chosen = {}
            for rank, bit in enumerate(open_bits):
                chosen[bit] = (step // 2 ** (len(open_bits) - 1 - rank)) % 2
            full = [chosen.get(bit, mine[bit]) for bit in range(bits)]
            small = [full[bit] for bit in range(bits) if bit != order[0]]
            return tuple(full), tuple(small), tuple(chosen[bit] for bit in open_bits)

        def one(step, carry):
            full, small, inner = place(step)
            kept = sources[stream][full] if stage == 0 else held[stream][small]
            total = kept.astype(F32) + target[inner].astype(F32)
            if stage == bits - 1:
                results[stream][...] = total
            else:
                held[stream][small] = total.astype(BF16)
            return carry

        if open_bits:
            lax.fori_loop(0, 2 ** len(open_bits), one, 0)
        else:
            one(0, 0)

    for stream in range(streams):
        start(stream, 0)
    for stage in range(bits):
        for stream in range(streams):
            copies[stream, stage].wait_recv()
            add(stream, stage)
            if stage + 1 < bits:
                start(stream, stage + 1)
    for copy in copies.values():
        copy.wait_send()


def reduce_blocks(arrays, bit_counts, orders):
    bits = sum(bit_counts)
    shaped = [array.reshape((2,) * bits + array.shape[1:]) for array in arrays]
    streams = len(arrays)
    vmem = pl.BlockSpec(memory_space=pltpu.VMEM)
    held = [pltpu.VMEM((2,) * (bits - 1) + array.shape[1:], BF16) for array in arrays]
    landing = [
        pltpu.VMEM((2,) * (bits - 1 - stage) + array.shape[1:], BF16)
        for array in arrays
        for stage in range(bits)
    ]
    return pl.pallas_call(
        partial(reduce_kernel, bit_counts, orders),
        out_shape=[jax.ShapeDtypeStruct(array.shape[1:], F32) for array in arrays],
        in_specs=[vmem] * streams,
        out_specs=[vmem] * streams,
        scratch_shapes=held
        + landing
        + [pltpu.SemaphoreType.DMA((streams * bits,)), pltpu.SemaphoreType.DMA((streams * bits,))],
        compiler_params=pltpu.CompilerParams(collective_id=2, has_side_effects=True),
        name="reduce_blocks",
    )(*shaped)


def split_product(left, right):
    high = left.astype(BF16)
    low = (left - high.astype(F32)).astype(BF16)
    both = jnp.concatenate([high, low], axis=0)
    product = jnp.einsum("sd,ed->se", both, right, preferred_element_type=F32)
    return product[: left.shape[0]] + product[left.shape[0] :]


def route(owners, embed_grad, seq_count, capacity):
    onehot = (owners[:, None] == jnp.arange(seq_count, dtype=jnp.int32)[None, :]).astype(BF16)
    tokens = owners.shape[0]
    earlier = (jnp.arange(tokens)[:, None] > jnp.arange(tokens)[None, :]).astype(BF16)
    before = jnp.dot(earlier, onehot, preferred_element_type=F32)
    rank = jnp.sum(before * onehot.astype(F32), axis=1).astype(jnp.int32)
    slot_index = owners * capacity + rank
    selector = (
        jnp.arange(seq_count * capacity, dtype=jnp.int32)[:, None] == slot_index[None, :]
    ).astype(BF16)
    outgoing = jnp.dot(selector, embed_grad, preferred_element_type=F32).astype(BF16)
    return outgoing.reshape(seq_count, capacity, embed_grad.shape[1])


def local_by_head(
    tile_embed,
    qkv_saved,
    out_cotangent,
    qkv_weight,
    out_weight,
    seg_length,
    dilation,
    owner_map,
    tile_hidden,
    tile_output,
    embed_weight,
    proj_weight,
):
    head_count = seg_length.shape[0]
    heads_width = out_weight.shape[0]
    width = heads_width // head_count
    tokens = qkv_saved.shape[1]
    seq_count = lax.axis_size("seq")
    dp_count = lax.axis_size("dp")
    devices = seq_count * dp_count
    bit_counts = (dp_count.bit_length() - 1, seq_count.bit_length() - 1)
    length = tokens * seq_count
    cotangent, embed_rows = out_cotangent[0], tile_embed[0]
    grads_out = jnp.einsum("cd,td->ct", out_weight, cotangent, preferred_element_type=F32)
    blocks = jnp.concatenate([qkv_saved[0].T, grads_out.astype(BF16)], axis=0)
    blocks = blocks.reshape(4, head_count, width, tokens).transpose(1, 0, 2, 3)
    blocks = blocks.reshape(head_count, 4 * width, tokens)
    head = lax.axis_index("seq")
    span = lax.dynamic_index_in_dim(seg_length, head, keepdims=False)
    stride = lax.dynamic_index_in_dim(dilation, head, keepdims=False)
    pos = jnp.arange(length, dtype=jnp.int32)
    ids = pos // span * stride + pos % stride
    returned = attention_by_head(blocks, ids, width, width ** (-0.5))
    parts = returned.reshape(head_count, 4, width, tokens).transpose(1, 0, 2, 3)
    attention = parts[0].reshape(heads_width, tokens)
    qkv_grad = parts[1:].reshape(3 * heads_width, tokens)
    embed_grad = (
        cotangent.astype(F32)
        + jnp.einsum("ct,dc->td", qkv_grad, qkv_weight, preferred_element_type=F32)
    ).astype(BF16)
    capacity = tile_hidden.shape[1] // seq_count
    incoming = exchange(route(owner_map[0, :, 0], embed_grad, seq_count, capacity))
    incoming = incoming.reshape(seq_count * capacity, embed_grad.shape[1])

    qkv_term = jnp.einsum("tc,kt->ck", embed_rows, qkv_grad, preferred_element_type=F32)
    out_term = jnp.einsum("ct,tk->ck", attention, cotangent, preferred_element_type=F32)
    qkv_rows = qkv_weight.shape[0] // devices
    out_rows = heads_width // devices
    qkv_cols = qkv_weight.shape[1]
    packed = out_rows * out_weight.shape[1] // qkv_cols
    slide_terms = jnp.concatenate(
        [
            qkv_term.astype(BF16).reshape(devices, qkv_rows, qkv_cols),
            out_term.astype(BF16).reshape(devices, packed, qkv_cols),
        ],
        axis=1,
    )
    embed_term = jnp.einsum("sc,sd->cd", tile_output[0], incoming, preferred_element_type=F32)
    factor_term = jnp.einsum("sc,sd->cd", tile_hidden[0], incoming, preferred_element_type=F32)
    tile_rows = embed_weight.shape[0] // devices
    tile_shape = (devices, tile_rows, embed_weight.shape[1])
    tile_grad = jnp.einsum("sd,ed->se", incoming, embed_weight, preferred_element_type=F32)
    hidden_grad = jnp.einsum(
        "se,fe->sf", tile_grad.astype(BF16), proj_weight, preferred_element_type=F32
    ).astype(BF16)[None]
    dp_bits, bits = bit_counts[0], sum(bit_counts)
    core = dp_bits - 1
    high = list(range(dp_bits - 1))
    low = list(range(dp_bits, bits))
    orders = (
        [core] + high + low[::-1],
        [core] + low[::-1][:1] + high + low[::-1][1:],
        [core] + low[1:2] + high + low[2:] + low[:1],
    )
    slide_sum, embed_sum, factor = reduce_blocks(
        [
            slide_terms,
            embed_term.astype(BF16).reshape(tile_shape),
            factor_term.astype(BF16).reshape(tile_shape),
        ],
        bit_counts,
        orders,
    )
    proj_sum = split_product(factor, embed_weight)
    qkv_sum = slide_sum[:qkv_rows]
    out_sum = slide_sum[qkv_rows:].reshape(out_rows, out_weight.shape[1])
    return (hidden_grad, proj_sum, embed_sum, qkv_sum, out_sum)


def pick(*args):
    head_count = args[5].shape[0]
    heads_width = args[4].shape[0]
    seq_count, dp_count = lax.axis_size("seq"), lax.axis_size("dp")
    devices = seq_count * dp_count
    fits = head_count == seq_count and (heads_width // head_count) % 16 == 0
    fits = fits and dp_count > 1 and devices & (devices - 1) == 0
    fits = fits and args[10].shape[0] % (16 * devices) == 0
    fits = fits and (heads_width * args[4].shape[1]) % (devices * args[3].shape[1]) == 0
    return local_by_head(*args) if fits else local(*args)


def solution(mesh):
    return jax.shard_map(
        pick,
        mesh=mesh,
        in_specs=(
            P("dp", "seq", None),
            P("dp", "seq", None),
            P("dp", "seq", None),
            P(),
            P(),
            P(),
            P(),
            P("dp", "seq", None),
            P("dp", "seq", None),
            P("dp", "seq", None),
            P(),
            P(),
        ),
        out_specs=(
            P("dp", "seq", None),
            P(("dp", "seq"), None),
            P(("dp", "seq"), None),
            P(("dp", "seq"), None),
            P(("dp", "seq"), None),
        ),
        check_vma=False,
    )
```
